512 devices in a mesh: expert: 8 (over x, core), tensor: 64 (over y, z).
Axes of the slice: x: 4, y: 8, z: 8, core: 2. Of those that a mesh axis runs over, the one named last changes fastest.
Arguments:
- tokens: bfloat16 [1536, 6144], P('tensor'), may hold values from -6 to 6
- expert_ids: int32 [1536, 2], P('tensor'), may hold values from 0 to 7, all different within a row; in each aligned block of 24 rows (0 to 23, 24 to 47, ...) at most 12 rows name the same one
- gate_units: int32 [1536, 2], P('tensor'), may hold values from 1 to 65535
- gate_weight: bfloat16 [8, 6144, 8192], P('expert', None, 'tensor'), may hold values from -0.078125 to 0.078125
- up_weight: bfloat16 [8, 6144, 8192], P('expert', None, 'tensor'), may hold values from -0.078125 to 0.078125
- down_weight: bfloat16 [8, 6144, 8192], P('expert', 'tensor'), may hold values from -0.0625 to 0.0625
Outputs:
- expert_mix: bfloat16 [1536, 6144], P('tensor', 'expert')
The draws below stay inside these ranges and needn't reach their ends.
Inputs may be any that keep to these rules, and one draw needn't show every extreme that they name: `expert_ids`: within each aligned block of 24 rows (the tokens of one tensor index) the two ids of a row differ and no expert is named by more than 12 rows; in every draw some expert is named by exactly 12 rows of some block, and every expert is named somewhere.
All inputs are finite; a program needn't handle non-finite values.
Results may differ from the reference program's by a relative error of at most 0.0057.
Values may be sent and summed in bfloat16 or wider, within the bound.
A program may use at most 128 MiB of HBM per device.

```python
import math
import jax
import jax.numpy as jnp
import numpy as np
from jax import lax

D = 6144
FF = 8192
TOPK = 2
TOK_T = 24
EXPERTS = 8
CAPT = 12
TOKENS = 1536
N_TENSOR = 64


def set_ends(result, own_key, smallest, top_value):
    shape = result.shape
    place = [jax.random.randint(jax.random.fold_in(own_key, axis), (), 0, shape[axis]) for axis in range(len(shape))]
    result = result.at[tuple(place)].set(smallest)
    longest = shape.index(max(shape))
    place[longest] = (place[longest] + 1) % shape[longest]
    return result.at[tuple(place)].set(top_value)


def level_of(own_key, dims, cuts, least, largest):
    def one(dim, blocks):
        draws = jax.random.uniform(jax.random.fold_in(jax.random.fold_in(own_key, 6), dim), (blocks,), jnp.float32, least / len(cuts), largest / len(cuts))
        return jnp.repeat(jnp.exp(draws), dims[dim] // blocks).reshape((-1,) + (1,) * (len(dims) - dim - 1))

    loudness = one(*cuts[0])
    for cut in cuts[1:]:
        loudness = loudness * one(*cut)
    return loudness


def deal_out(key, own, number, rows, amount, top, limit, skew):
    sequence = jax.random.permutation(key, amount)
    heavy_load, usual = load_shares(amount, rows * top, limit, skew, True), load_shares(amount, rows * top, limit, skew, False)
    places = jnp.arange(amount)

    def named(lengths, offset_by):
        used = int((lengths > 0).sum())
        fixed = max(1, used // 4)
        moved = fixed + (places - fixed + offset_by * (used - fixed)) % max(1, amount - fixed)
        return jnp.zeros((amount,), jnp.int32).at[sequence[jnp.where(places < fixed, places, moved)]].set(jnp.asarray(lengths, jnp.int32))

    lengths = jnp.where(number % 4 == 0, named(heavy_load, number // 4), named(usual, number - number // 4 - 1))
    mixed = jax.random.permutation(jax.random.fold_in(own, 3), amount)
    donor, receiver = mixed[0:amount // 2 * 2:2], mixed[1:amount // 2 * 2:2]
    margin = jnp.minimum(lengths[donor] - 1, limit - lengths[receiver]) // 2
    margin = jnp.where((donor == sequence[0]) | (receiver == sequence[0]) | (lengths[receiver] == 0), 0, jnp.maximum(margin, 0))
    moved = jax.random.randint(jax.random.fold_in(own, 4), (amount // 2,), 0, 1 << 20) % (margin + 1)
    lengths = lengths.at[donor].add(-moved).at[receiver].add(moved)
    members = jnp.searchsorted(jnp.cumsum(lengths), jnp.arange(rows * top), side="right").astype(jnp.int32)
    table = members.reshape(top, rows).T
    table = table[jax.random.permutation(jax.random.fold_in(own, 1), rows)]
    offset_by = jax.random.randint(jax.random.fold_in(own, 2), (rows, 1), 0, top)
    return jnp.take_along_axis(table, (jnp.arange(top)[None, :] + offset_by) % top, axis=1)


def load_shares(amount, total, bound, lean, full):
    loads = [(1 << 20) // math.isqrt(standing ** lean) + 1 for standing in range(1, amount + 1)]
    largest = bound if full else min(bound, max(-(-total // amount), total * loads[0] // sum(loads)))
    least = 1 if total - largest >= amount - 1 else 0
    counts, spare = [largest] + [least] * (amount - 1), total - largest - least * (amount - 1)
    while spare > 0:
        candidates = [i for i in range(1, amount) if counts[i] < largest] or [i for i in range(1, amount) if counts[i] < bound]
        whole, remaining = sum([loads[i] for i in candidates]), spare
        for i in candidates:
            addition = min(bound - counts[i], max(1, remaining * loads[i] // whole), spare)
            counts[i] = counts[i] + addition
            spare = spare - addition
    return np.array(counts)


def noise(stream_key, shape, width, bound, cuts=(), kind=jnp.bfloat16):
    level = level_of(stream_key, shape, cuts, -0.22, 0.18) if cuts else 1.0
    drawn = jax.random.normal(stream_key, shape, jnp.float32) * width * level
    return jnp.minimum(jnp.maximum(drawn, -bound), bound).astype(kind)


def setup_inputs(seed: int = 0) -> dict:
    splits = jax.random.split(jax.random.key(seed), 7)
    tokens = noise(splits[0], (TOKENS, D), 1.0, 6.0, ((0, 64),))
    expert_ids_keys = jax.random.split(jax.random.fold_in(splits[1], 1), TOKENS // TOK_T)
    expert_ids_turns = jax.random.permutation(jax.random.fold_in(splits[1], 3), TOKENS // TOK_T)
    expert_ids = jax.vmap(lambda own, number: deal_out(jax.random.fold_in(splits[1], 2), own, number, TOK_T, EXPERTS, TOPK, CAPT, 2))(expert_ids_keys, expert_ids_turns).reshape((TOKENS, TOPK))
    gate_units = set_ends(jax.random.randint(splits[2], (TOKENS, TOPK), 1, 65536), jax.random.fold_in(splits[2], 1), 1, 65535).astype(jnp.int32)
    gate_weight = noise(splits[3], (EXPERTS, D, FF), D ** -0.5, 0.078125, ((0, 8), (2, 64)))
    up_weight = noise(splits[4], (EXPERTS, D, FF), D ** -0.5, 0.078125, ((0, 8), (2, 64)))
    down_weight = noise(splits[5], (EXPERTS, D, FF), FF ** -0.5, 0.0625, ((0, 8), (1, 64)))
    return {"tokens": tokens, "expert_ids": expert_ids, "gate_units": gate_units, "gate_weight": gate_weight, "up_weight": up_weight, "down_weight": down_weight}


def slot_tables(expert_ids, gate_units, expert_id, capacity):
    tok_rows = expert_ids.shape[0]
    top_count = expert_ids.shape[1]
    flat_route = expert_ids.reshape(-1)
    matches = (flat_route == expert_id).astype(jnp.int32)
    slot_rank = jnp.cumsum(matches) - matches
    slot_ids = jnp.arange(capacity, dtype=jnp.int32)
    assignment = jnp.where((slot_rank[None, :] == slot_ids[:, None]) & (matches[None, :] == 1), 1.0, 0.0).astype(jnp.float32)
    positions = jnp.arange(tok_rows * top_count, dtype=jnp.int32) // top_count
    owners = (positions[:, None] == jnp.arange(tok_rows, dtype=jnp.int32)[None, :]).astype(jnp.float32)
    unit_vals = gate_units.astype(jnp.float32)
    shares = unit_vals / jnp.sum(unit_vals, axis=1, keepdims=True)
    picker = jnp.dot(assignment, owners, precision=lax.Precision.HIGHEST, preferred_element_type=jnp.float32)
    weighted = jnp.dot(assignment, owners * shares.reshape(-1)[:, None], precision=lax.Precision.HIGHEST, preferred_element_type=jnp.float32)
    return picker, weighted


def reference(tokens, expert_ids, gate_units, gate_weight, up_weight, down_weight):
    block_ids = expert_ids.reshape(N_TENSOR, TOK_T, TOPK)
    block_units = gate_units.reshape(N_TENSOR, TOK_T, TOPK)
    block_tokens = tokens.reshape(N_TENSOR, TOK_T, D).astype(jnp.float32)

    def one_expert(summed, expert_id):
        picker, weighted = jax.vmap(lambda ids, units: slot_tables(ids, units, expert_id, CAPT))(block_ids, block_units)
        picked = jnp.einsum("bct,btd->bcd", picker, block_tokens, precision=lax.Precision.HIGHEST).astype(jnp.bfloat16)
        picked = picked.reshape(N_TENSOR * CAPT, D)
        gate_vals = jnp.dot(picked, gate_weight[expert_id], preferred_element_type=jnp.float32)
        up_vals = jnp.dot(picked, up_weight[expert_id], preferred_element_type=jnp.float32)
        hidden = (jax.nn.silu(gate_vals) * up_vals).astype(jnp.bfloat16)
        projected = jnp.dot(hidden, down_weight[expert_id].T, preferred_element_type=jnp.float32).astype(jnp.bfloat16)
        returned = projected.reshape(N_TENSOR, CAPT, D).astype(jnp.float32)
        contribution = jnp.einsum("bct,bcd->btd", weighted, returned, precision=lax.Precision.HIGHEST)
        return summed + contribution.reshape(TOKENS, D), None

    start_sum = jnp.zeros((TOKENS, D), jnp.float32)
    summed, unused = lax.scan(one_expert, start_sum, jnp.arange(EXPERTS, dtype=jnp.int32))
    return summed.astype(jnp.bfloat16)
```

```python
import functools

import jax
import jax.numpy as jnp
from jax import lax
from jax.experimental import pallas as pl
from jax.experimental.pallas import tpu as pltpu
from jax.sharding import PartitionSpec as P

MESH = pl.DeviceIdType.MESH
R = 8
NX = 4
PIECE = 1536
WIDE = PIECE + 128
ROWS = 96
SLOTS = 768
HALF = 48
F32, BF16 = jnp.float32, jnp.bfloat16


def mod(a, n):
    return lax.rem(a + 4 * n, n)


def kernel(own_ref, wg_ref, wu_ref, wd_ref, wall_ref, out_ref,
           ph1, xin, xo, wgu, wab, hacc, hg, psend, precv, sumt, fsend, frecv,
           loc, r1, s1, r2, s2, rx, sx, rs, ss, wr, ws, hr, hs, pr, ps, fr, fs):
    e, t = lax.axis_index("expert"), lax.axis_index("tensor")
    y, z = t // R, lax.rem(t, R)
    x, c = e // 2, lax.rem(e, 2)
    d = 1 - 2 * c
    pos1, pos2 = (z, y), (y, z)
    sib = x * 2 + 1 - c
    xdev = (mod(x + 1, NX) * 2 + c, mod(x - 1, NX) * 2 + c)
    quarter = lax.rem(x, 2) * 2 + c

    def on_z(p):
        return (e, y * R + mod(p, R))

    def on_y(p):
        return (e, mod(p, R) * R + z)

    dev1, dev2 = (on_z, on_y), (on_y, on_z)

    def remote(src, dst, send, recv, dev):
        return pltpu.make_async_remote_copy(
            src_ref=src, dst_ref=dst, send_sem=send, recv_sem=recv,
            device_id=dev, device_id_type=MESH)

    def waiter(ref, sem):
        return pltpu.make_async_copy(ref, ref, sem)

    loads = [pltpu.make_async_copy(wg_ref, wgu.at[:, pl.ds(0, 128)], loc.at[0]),
             pltpu.make_async_copy(wu_ref, wgu.at[:, pl.ds(128, 128)], loc.at[1])]
    for k in (0, 1):
        loads.append(pltpu.make_async_copy(own_ref.at[k], ph1.at[k, pos1[k]], loc.at[2 + k]))
    for one in loads:
        one.start()

    barrier = pltpu.get_barrier_semaphore()

    @pl.loop(1, R)
    def _(k):
        pl.semaphore_signal(barrier, inc=1, device_id=on_z(z + k), device_id_type=MESH)
        pl.semaphore_signal(barrier, inc=1, device_id=on_y(y + k), device_id_type=MESH)

    for dev in (xdev[0], xdev[1], sib):
        pl.semaphore_signal(barrier, inc=1, device_id=(dev, t), device_id_type=MESH)
    pl.semaphore_wait(barrier, 2 * (R - 1) + 3)

    def travel(s):
        way = (2 * lax.rem(s, 2) - 1) * d
        return way, (s + 1) // 2

    for k in (0, 1):
        me = pos1[k]
        remote(own_ref.at[k], ph1.at[k, me], s1.at[k, 0], r1.at[k, 1], dev1[k](me + d)).start()
        remote(own_ref.at[k], ph1.at[k, me], s1.at[k, 1], r1.at[k, 2], dev1[k](me - d)).start()

    @pl.loop(1, R)
    def _(s):
        way, far = travel(s)
        for k in (0, 1):
            blk = ph1.at[k, mod(pos1[k] - way * far, R)]
            waiter(blk, r1.at[k, s]).wait()

            @pl.when(s <= 5)
            def _():
                remote(blk, blk, s1.at[k, s + 1], r1.at[k, s + 2], dev1[k](pos1[k] + way)).start()

    for one in loads:
        one.wait()

    row = lax.broadcasted_iota(jnp.int32, (ROWS, 128), 0)
    col = lax.broadcasted_iota(jnp.int32, (ROWS, 128), 1)
    take = jnp.where(col == (row // 12) * 16 + lax.rem(row, 12), 1.0, 0.0).astype(BF16)
    for k in (0, 1):
        xin[k, pos2[k]] = jnp.dot(take, ph1[k].reshape(128, WIDE), preferred_element_type=F32).astype(BF16)

    def share(k, g, s):
        src = xin.at[k, g, :, pl.ds(0, PIECE)]
        remote(src, xo.at[k, 1, g], sx.at[k, s], rx.at[k, s], (xdev[k], t)).start()
        remote(src, xo.at[k, 0, g], ss.at[k, 0, s], rs.at[k, 0, s], (sib, t)).start()

    for k in (0, 1):
        me = pos2[k]
        blk = xin.at[k, me]
        remote(blk, blk, s2.at[k, 0], r2.at[k, 1], dev2[k](me + d)).start()
        remote(blk, blk, s2.at[k, 1], r2.at[k, 2], dev2[k](me - d)).start()
        share(k, me, 0)

    def arrive(s):
        way, far = travel(s)
        for k in (0, 1):
            g = mod(pos2[k] - way * far, R)
            blk = xin.at[k, g]
            waiter(blk, r2.at[k, s]).wait()

            @pl.when(s <= 5)
            def _():
                remote(blk, blk, s2.at[k, s + 1], r2.at[k, s + 2], dev2[k](pos2[k] + way)).start()

            share(k, g, s)

    def weights(k):
        ty, tz = mod(y + k, R), mod(z + k, R)
        remote(wd_ref.at[pl.ds(0, HALF), pl.ds(pl.multiple_of(ty * 1024, 1024), 1024)],
               wab.at[0, y], ws.at[0], wr.at[0], on_y(ty)).start()
        for j in range(R):
            remote(wd_ref.at[pl.ds(HALF, HALF), pl.ds(pl.multiple_of(j * 1024 + tz * 128, 128), 128)],
                   wab.at[1, z, :, pl.ds(j * 128, 128)], ws.at[1], wr.at[1], on_z(tz)).start()

    pltpu.make_async_copy(wd_ref.at[pl.ds(0, HALF), pl.ds(pl.multiple_of(y * 1024, 1024), 1024)],
                          wab.at[0, y], wr.at[0]).start()
    for j in range(R):
        pltpu.make_async_copy(wd_ref.at[pl.ds(HALF, HALF), pl.ds(pl.multiple_of(j * 1024 + z * 128, 128), 128)],
                              wab.at[1, z, :, pl.ds(j * 128, 128)], wr.at[1]).start()

    hacc[...] = jnp.zeros_like(hacc)

    def relay(s):
        way, far = travel(s)
        for k in (0, 1):
            g = mod(pos2[k] - way * far, R)
            blk = xo.at[k, 1, g]
            waiter(blk, rx.at[k, s]).wait()
            remote(blk, xo.at[k, 2, g], ss.at[k, 1, s], rs.at[k, 1, s], (sib, t)).start()

    def multiply(s):
        way, far = travel(s)
        even = lax.rem(s, 2) == 0
        other = jnp.where((s == 0) | (s == 7), s, jnp.where(even, s - 1, s + 1))

        for k in (0, 1):
            g = mod(pos2[k] - way * far, R)
            for j in (0, 1):
                waiter(xo.at[k, 2 * j, g], rs.at[k, j, other]).wait()

            def part(rows, q):
                first = pl.multiple_of(q * PIECE, PIECE)
                return jnp.dot(rows, wgu[pl.ds(first, PIECE), :], preferred_element_type=F32)

            acc = part(xin[k, g, :, pl.ds(0, PIECE)], quarter)
            acc += part(xo[k, 0, g], quarter + 1 - 2 * c)
            acc += part(xo[k, 1, g], lax.rem(quarter + 2, 4))
            acc += part(xo[k, 2, g], lax.rem(quarter + 2, 4) + 1 - 2 * c)
            gate, up = acc[:, :128], acc[:, 128:]
            hidden = (gate / (1.0 + jnp.exp(-gate)) * up).astype(BF16)
            slot = xin[k, g, :, pl.ds(PIECE, 128)].astype(F32)[:, 0:1]
            line = lax.broadcasted_iota(jnp.int32, (ROWS, 1), 0) // 12
            block = g * R + line if k == 0 else line * R + g
            goal = jnp.where(slot >= 0, block.astype(F32) * 12.0 + slot, -1.0)
            place = lax.broadcasted_iota(jnp.int32, (ROWS, SLOTS), 1).astype(F32)
            chosen = jnp.where(place == goal, 1.0, 0.0).astype(BF16)
            hacc[...] += lax.dot_general(chosen, hidden, (((0,), (0,)), ((), ())), preferred_element_type=F32)

    arrive(jnp.int32(1))

    @pl.loop(0, R + 1)
    def _(s):
        @pl.when(s + 2 < R)
        def _():
            arrive(s + 2)

        @pl.when(s + 1 < R)
        def _():
            weights(s + 1)

        @pl.when(s < R)
        def _():
            relay(s)

        @pl.when(s > 0)
        def _():
            multiply(s - 1)

    H2 = SLOTS // 2
    hpos, hdev = (z, y), (on_z, on_y)

    def piece(k, p, h):
        return hg.at[k, pl.ds(h * H2, H2), pl.ds(pl.multiple_of(mod(p, R) * 128, 128), 128)]

    done = hacc[...].astype(BF16)
    for k in (0, 1):
        hg[k, :, pl.ds(pl.multiple_of(hpos[k] * 128, 128), 128)] = done
    for h in (0, 1):
        for k in (0, 1):
            blk = piece(k, hpos[k], h)
            remote(blk, blk, hs.at[k, h, 0], hr.at[k, h, 1], hdev[k](hpos[k] + d)).start()
            remote(blk, blk, hs.at[k, h, 1], hr.at[k, h, 2], hdev[k](hpos[k] - d)).start()

    @pl.loop(1, R)
    def _(s):
        way, far = travel(s)
        for h in (0, 1):
            for k in (0, 1):
                blk = piece(k, hpos[k] - way * far, h)
                waiter(blk, hr.at[k, h, s]).wait()

                @pl.when(s <= 5)
                def _():
                    remote(blk, blk, hs.at[k, h, s + 1], hr.at[k, h, s + 2], hdev[k](hpos[k] + way)).start()

    for k in (0, 1):
        waiter(wab.at[k], wr.at[k]).wait()

    ppos, pdev = (y, z), (on_y, on_z)
    for k in (0, 1):
        @pl.loop(0, 3)
        def _(n):
            cols = pl.ds(pl.multiple_of(n * 256, 256), 256)
            part = lax.dot_general(wab[k].reshape(R * HALF, 1024), hg[k, cols, :], (((1,), (1,)), ((), ())),
                                   preferred_element_type=F32)
            psend[k, :, :, cols] = part.astype(BF16).reshape(R, HALF, 256)

        @pl.loop(1, R)
        def _(j):
            to = mod(ppos[k] + j, R)
            remote(psend.at[k, to], precv.at[k, ppos[k]], ps.at[k], pr.at[k], pdev[k](to)).start()

    sumt[...] = jnp.zeros_like(sumt)
    for k in (0, 1):
        waiter(precv.at[k, pl.ds(0, R - 1)], pr.at[k]).wait()
        precv[k, ppos[k]] = psend[k, ppos[k]]
        total = precv[k, 0].astype(F32)
        for j in range(1, R):
            total += precv[k, j].astype(F32)
        sumt[pl.ds(k * HALF, HALF), :] = total.astype(BF16)

    @pl.loop(0, 4)
    def _(n):
        r = lax.broadcasted_iota(jnp.int32, (256, SLOTS), 0) + n * 256
        at = lax.rem(r, 16)
        goal = jnp.where(at < 12, (r // 16) * 12 + at, -1)
        order = jnp.where(lax.broadcasted_iota(jnp.int32, (256, SLOTS), 1) == goal, 1.0, 0.0).astype(BF16)
        got = lax.dot_general(order, sumt[...], (((1,), (1,)), ((), ())), preferred_element_type=F32)
        fsend[pl.ds(n * 16, 16)] = got.astype(BF16).reshape(16, 16, 128)

    mine = e == y
    landing = frecv.at[z * R + e]

    @pl.loop(0, R * R)
    def _(b):
        here = jnp.logical_and(b == t, mine)

        @pl.when(here)
        def _():
            pltpu.make_async_copy(fsend.at[b], landing, fr).start()

        @pl.when(jnp.logical_not(here))
        def _():
            remote(fsend.at[b], landing, fs, fr, (y, b)).start()

    waiter(frecv, fr).wait()
    for n in range(R):
        got = frecv[pl.ds(n * R, R)].reshape(128, 128).astype(F32)
        mixed = jnp.dot(wall_ref[...], got, precision=lax.Precision.HIGHEST, preferred_element_type=F32)
        out_ref[:, pl.ds(n * 128, 128)] = mixed.astype(BF16)

    @pl.loop(0, R - 1)
    def _(s):
        for k in (0, 1):
            waiter(ph1.at[k, 0], s1.at[k, s]).wait()
            waiter(xin.at[k, 0], s2.at[k, s]).wait()
            for h in (0, 1):
                waiter(piece(k, 0, h), hs.at[k, h, s]).wait()

    @pl.loop(0, R)
    def _(s):
        for k in (0, 1):
            waiter(xo.at[k, 0, 0], sx.at[k, s]).wait()
            for j in (0, 1):
                waiter(xo.at[k, 0, 0], ss.at[k, j, s]).wait()

    for k in (0, 1):
        waiter(wab.at[k, pl.ds(0, R - 1)], ws.at[k]).wait()
        waiter(psend.at[k, pl.ds(0, R - 1)], ps.at[k]).wait()

    @pl.when(mine)
    def _():
        waiter(fsend.at[pl.ds(0, R * R - 1)], fs).wait()

    @pl.when(jnp.logical_not(mine))
    def _():
        waiter(fsend, fs).wait()


def local(tokens, expert_ids, gate_units, gate_weight, up_weight, down_weight):
    e = lax.axis_index("expert")
    quarter = lax.rem(e // 2, 2) * 2 + lax.rem(e, 2)
    rows = tokens.shape[0]
    flat = expert_ids.reshape(-1)
    before = jnp.arange(2 * rows)[None, :] < jnp.arange(2 * rows)[:, None]
    rank = jnp.sum(jnp.where(before & (flat[None, :] == flat[:, None]), 1, 0), axis=1).reshape(rows, 2)
    slot = jnp.sum(jnp.where(expert_ids == e, rank + 1, 0), axis=1) - 1
    units = gate_units.astype(F32)
    shares = units / jnp.sum(units, axis=1, keepdims=True)
    lane = jnp.arange(128)[None, :]
    goal = expert_ids * 16 + rank
    wall = jnp.where(lane == goal[:, 0:1], shares[:, 0:1], 0.0) + jnp.where(lane == goal[:, 1:2], shares[:, 1:2], 0.0)
    mine = lax.dynamic_slice_in_dim(tokens, quarter * PIECE, PIECE, 1)
    tag = jnp.broadcast_to(slot[:, None].astype(BF16), (rows, 128))
    own = jnp.concatenate([mine, tag], axis=1).reshape(2, 12, WIDE)
    own = jnp.pad(own, ((0, 0), (0, 4), (0, 0)))

    dma = pltpu.SemaphoreType.DMA
    anywhere = pl.BlockSpec(memory_space=pl.ANY)
    vmem = pl.BlockSpec(memory_space=pltpu.VMEM)
    out = pl.pallas_call(
        kernel,
        out_shape=jax.ShapeDtypeStruct((rows, 1024), BF16),
        in_specs=[vmem, anywhere, anywhere, anywhere, vmem],
        out_specs=vmem,
        scratch_shapes=[
            pltpu.VMEM((2, R, 16, WIDE), BF16),
            pltpu.VMEM((2, R, ROWS, WIDE), BF16),
            pltpu.VMEM((2, 3, R, ROWS, PIECE), BF16),
            pltpu.VMEM((4 * PIECE, 256), BF16),
            pltpu.VMEM((2, R, HALF, 1024), BF16),
            pltpu.VMEM((SLOTS, 128), F32),
            pltpu.VMEM((2, SLOTS, 1024), BF16),
            pltpu.VMEM((2, R, HALF, SLOTS), BF16),
            pltpu.VMEM((2, R, HALF, SLOTS), BF16),
            pltpu.VMEM((128, SLOTS), BF16),
            pltpu.VMEM((R * R, 16, 128), BF16),
            pltpu.VMEM((R * R, 16, 128), BF16),
            dma((4,)),
            dma((2, R)), dma((2, R)),
            dma((2, R)), dma((2, R)),
            dma((2, R)), dma((2, R)),
            dma((2, 2, R)), dma((2, 2, R)),
            dma((2,)), dma((2,)),
            dma((2, 2, R)), dma((2, 2, R)),
            dma((2,)), dma((2,)),
            dma, dma,
        ],
        compiler_params=pltpu.CompilerParams(
            collective_id=0, has_side_effects=True, vmem_limit_bytes=60 * 1024 * 1024),
    )(own, gate_weight[0], up_weight[0], down_weight[0], wall)
    return out.reshape(rows, R, 128)[:, :, :HALF * 2].reshape(rows, R * HALF * 2)


def solution(mesh):
    return jax.shard_map(
        local,
        mesh=mesh,
        in_specs=(
            P("tensor", None),
            P("tensor", None),
            P("tensor", None),
            P("expert", None, "tensor"),
            P("expert", None, "tensor"),
            P("expert", "tensor", None),
        ),
        out_specs=P("tensor", "expert"),
        check_vma=False,
    )
```

```python
import jax
import jax.numpy as jnp
from jax import lax
from jax.experimental import pallas as pl
from jax.experimental.pallas import tpu as pltpu
from jax.sharding import PartitionSpec as P

MESH = pl.DeviceIdType.MESH
R = 8
NX = 4
D = 6144
PIECE = 1408
BOTH = 256
OWN = PIECE + BOTH
WIDE = OWN + 128
ROWS = 96
CUT = ROWS // 2
SLOTS = 768
HS = SLOTS // 2
HALF = 48
F32, BF16 = jnp.float32, jnp.bfloat16


def mod(a, n):
    return lax.rem(a + 4 * n, n)


def iota(shape, axis):
    return lax.broadcasted_iota(jnp.int32, shape, axis)


def ones(test):
    return jnp.where(test, 1.0, 0.0)


def across(a, b, **how):
    return lax.dot_general(a, b, (((1,), (1,)), ((), ())), preferred_element_type=F32, **how)


def kernel(tok_ref, ids_ref, unit_ref, wg_ref, wu_ref, wd_ref, out_ref,
           ph1, phx, xin, xs, xx, wgu, wab, hacc, hg, psend, precv, sumt, order, wall, fsend, frecv,
           loc, r1, s1, x1, y1, r2, s2, rx, sx, rs, ss, rq, sq, wr, ws, hr, hs, pr, ps, fr, fs):
    e, t = lax.axis_index("expert"), lax.axis_index("tensor")
    y, z = t // R, lax.rem(t, R)
    x, c = e // 2, lax.rem(e, 2)
    d = 1 - 2 * c
    pos1, pos2 = (z, y), (y, z)
    sib = x * 2 + 1 - c
    xdev = (mod(x + 1, NX) * 2 + c, mod(x - 1, NX) * 2 + c)
    quarter = lax.rem(x, 2) * 2 + c

    def on_z(p):
        return (e, y * R + mod(p, R))

    def on_y(p):
        return (e, mod(p, R) * R + z)

    dev1, dev2 = (on_z, on_y), (on_y, on_z)

    def remote(src, dst, send, recv, dev):
        return pltpu.make_async_remote_copy(
            src_ref=src, dst_ref=dst, send_sem=send, recv_sem=recv,
            device_id=dev, device_id_type=MESH)

    def waiter(ref, sem):
        return pltpu.make_async_copy(ref, ref, sem)

    barrier = pltpu.get_barrier_semaphore()
    for dev in (on_z(z + 1), on_z(z - 1), on_y(y + 1), on_y(y - 1), (xdev[0], t), (xdev[1], t), (sib, t)):
        pl.semaphore_signal(barrier, inc=1, device_id=dev, device_id_type=MESH)

    first = pl.multiple_of(quarter * PIECE, 128)
    second = pl.multiple_of(4 * PIECE + c * BOTH, 128)
    blocks = []
    for k in (0, 1):
        rows = pl.ds(8 * k, 16)
        blocks.append(pltpu.make_async_copy(
            tok_ref.at[rows, pl.ds(first, PIECE)], ph1.at[k, pos1[k], :, pl.ds(0, PIECE)], loc.at[2 + k]))
        blocks.append(pltpu.make_async_copy(
            tok_ref.at[rows, pl.ds(second, BOTH)], ph1.at[k, pos1[k], :, pl.ds(PIECE, BOTH)], loc.at[4 + k]))
    loads = [pltpu.make_async_copy(wg_ref, wgu.at[:, pl.ds(0, 128)], loc.at[0]),
             pltpu.make_async_copy(wu_ref, wgu.at[:, pl.ds(128, 128)], loc.at[1])]
    for one in blocks + loads:
        one.start()

    tokens = ids_ref.shape[1]
    ids, units = ids_ref[...], unit_ref[...].astype(F32)
    shares = units / (units[0:1, :] + units[1:2, :])
    home = iota((128, tokens), 0) // 16
    named = (ones(home == ids[0:1, :]), ones(home == ids[1:2, :]))
    names = (named[0] + named[1]).astype(BF16)
    here, there = iota((tokens, tokens), 0), iota((tokens, tokens), 1)
    rank = across(ones(there < here).astype(BF16), names)
    used = across(ones(there == here).astype(BF16), names)
    weight = across(ones(there == here), named[0] * shares[0:1, :] + named[1] * shares[1:2, :],
                    precision=lax.Precision.HIGHEST)
    lane = iota((tokens, 128), 1)
    wall[...] = jnp.where(rank == lax.rem(lane, 16).astype(F32), weight, 0.0)
    slot = jnp.sum(jnp.where(lane == e * 16, jnp.where(used > 0.5, rank, -1.0), 0.0), axis=1, keepdims=True)
    tag = jnp.broadcast_to(slot, (tokens, 128))
    for k in (0, 1):
        ph1[k, pos1[k], :, pl.ds(OWN, 128)] = tag[8 * k:8 * k + 16].astype(BF16)

    for one in blocks:
        one.wait()
    pl.semaphore_wait(barrier, 7)

    def travel(s):
        way = (2 * lax.rem(s, 2) - 1) * d
        return way, (s + 1) // 2

    def early(k, p, s):
        remote(ph1.at[k, p, :, pl.ds(0, PIECE)], phx.at[k, p], y1.at[k, s], x1.at[k, s], (xdev[k], t)).start()

    for k in (0, 1):
        me = pos1[k]
        blk = ph1.at[k, me]
        remote(blk, blk, s1.at[k, 0], r1.at[k, 1], dev1[k](me + d)).start()
        remote(blk, blk, s1.at[k, 1], r1.at[k, 2], dev1[k](me - d)).start()
        early(k, me, 0)

    r = iota((512, HS), 0)
    at = lax.rem(r, 16)
    order[...] = ones(iota((512, HS), 1) == jnp.where(at < 12, (r // 16) * 12 + at, -1)).astype(BF16)

    @pl.loop(1, R)
    def _(s):
        way, far = travel(s)
        for k in (0, 1):
            p = mod(pos1[k] - way * far, R)
            blk = ph1.at[k, p]
            waiter(blk, r1.at[k, s]).wait()

            @pl.when(s <= 5)
            def _():
                remote(blk, blk, s1.at[k, s + 1], r1.at[k, s + 2], dev1[k](pos1[k] + way)).start()

            early(k, p, s)

    row, col = iota((ROWS, 128), 0), iota((ROWS, 128), 1)
    take = [ones(col == (row // 12) * 16 + 4 * k + lax.rem(row, 12)).astype(BF16) for k in (0, 1)]

    def share(k, g, s, h):
        rows = pl.ds(h * CUT, CUT)
        if s is not None:
            remote(xin.at[k, g, rows, pl.ds(0, PIECE)], xx.at[k, 0, g, rows], sx.at[k, h, s], rx.at[k, h, s],
                   (xdev[k], t)).start()
        s = 0 if s is None else s
        remote(xin.at[k, g, rows, pl.ds(0, OWN)], xs.at[k, g, rows], ss.at[k, h, s], rs.at[k, h, s], (sib, t)).start()

    for k in (0, 1):
        me = pos2[k]
        for h in (0, 1):
            blk = xin.at[k, me, pl.ds(h * CUT, CUT)]
            if h == 0:
                xin[k, me] = jnp.dot(take[k], ph1[k].reshape(128, WIDE), preferred_element_type=F32).astype(BF16)
            remote(blk, blk, s2.at[k, h, 0], r2.at[k, h, 1], dev2[k](me + d)).start()
            remote(blk, blk, s2.at[k, h, 1], r2.at[k, h, 2], dev2[k](me - d)).start()
    for k in (0, 1):
        for h in (0, 1):
            share(k, pos2[k], None, h)

    for one in loads:
        one.wait()

    def arrive(s):
        way, far = travel(s)
        for h in (0, 1):
            for k in (0, 1):
                g = mod(pos2[k] - way * far, R)
                blk = xin.at[k, g, pl.ds(h * CUT, CUT)]
                waiter(blk, r2.at[k, h, s]).wait()

                @pl.when(s <= 5)
                def _():
                    remote(blk, blk, s2.at[k, h, s + 1], r2.at[k, h, s + 2], dev2[k](pos2[k] + way)).start()

                share(k, g, s, h)

    def weights(k):
        ty, tz = mod(y + k, R), mod(z + k, R)
        remote(wd_ref.at[pl.ds(0, HALF), pl.ds(pl.multiple_of(ty * 1024, 1024), 1024)],
               wab.at[0, y], ws.at[0], wr.at[0], on_y(ty)).start()
        for j in range(R):
            remote(wd_ref.at[pl.ds(HALF, HALF), pl.ds(pl.multiple_of(j * 1024 + tz * 128, 128), 128)],
                   wab.at[1, z, :, pl.ds(j * 128, 128)], ws.at[1], wr.at[1], on_z(tz)).start()

    pltpu.make_async_copy(wd_ref.at[pl.ds(0, HALF), pl.ds(pl.multiple_of(y * 1024, 1024), 1024)],
                          wab.at[0, y], wr.at[0]).start()
    for j in range(R):
        pltpu.make_async_copy(wd_ref.at[pl.ds(HALF, HALF), pl.ds(pl.multiple_of(j * 1024 + z * 128, 128), 128)],
                              wab.at[1, z, :, pl.ds(j * 128, 128)], wr.at[1]).start()

    hacc[...] = jnp.zeros_like(hacc)

    def onward(k, g, s, h):
        blk = xx.at[k, 0, g, pl.ds(h * CUT, CUT)]
        remote(blk, xx.at[k, 1, g, pl.ds(h * CUT, CUT)], sq.at[k, h, s], rq.at[k, h, s], (sib, t)).start()

    def relay(s):
        way, far = travel(s)
        for h in (0, 1):
            for k in (0, 1):
                g = mod(pos2[k] - way * far, R)
                waiter(xx.at[k, 0, g, pl.ds(h * CUT, CUT)], rx.at[k, h, s]).wait()
                onward(k, g, s, h)

    def multiply(s):
        way, far = travel(s)
        even = lax.rem(s, 2) == 0
        other = jnp.where((s == 0) | (s == 7), s, jnp.where(even, s - 1, s + 1))

        for k in (0, 1):
            g = mod(pos2[k] - way * far, R)
            for h in (0, 1):
                waiter(xs.at[k, g, pl.ds(h * CUT, CUT)], rs.at[k, h, other]).wait()
                waiter(xx.at[k, 1, g, pl.ds(h * CUT, CUT)], rq.at[k, h, other]).wait()

            def part(rows, q, size=PIECE):
                return jnp.dot(rows, wgu[pl.ds(pl.multiple_of(q, 128), size), :], preferred_element_type=F32)

            beside, over = quarter + 1 - 2 * c, lax.rem(quarter + 2, 4)
            acc = part(xin[k, g, :, pl.ds(0, PIECE)], quarter * PIECE)
            acc += part(xin[k, g, :, pl.ds(PIECE, BOTH)], second, BOTH)
            acc += part(xs[k, g, :, pl.ds(0, PIECE)], beside * PIECE)
            acc += part(xs[k, g, :, pl.ds(PIECE, BOTH)], 4 * PIECE + (1 - c) * BOTH, BOTH)
            acc += part(xx[k, 0, g], over * PIECE)
            acc += part(xx[k, 1, g], (over + 1 - 2 * c) * PIECE)
            gate, up = acc[:, :128], acc[:, 128:]
            hidden = (gate / (1.0 + jnp.exp(-gate)) * up).astype(BF16)
            place = xin[k, g, :, pl.ds(OWN, 128)].astype(F32)[:, 0:1]
            line = iota((ROWS, 1), 0) // 12
            block = g * R + line if k == 0 else line * R + g
            goal = jnp.where(place >= 0, block.astype(F32) * 12.0 + place, -1.0)
            chosen = ones(iota((ROWS, SLOTS), 1).astype(F32) == goal).astype(BF16)
            hacc[...] += lax.dot_general(chosen, hidden, (((0,), (0,)), ((), ())), preferred_element_type=F32)

    arrive(jnp.int32(1))

    for k in (0, 1):
        @pl.loop(0, R)
        def _(s):
            waiter(phx.at[k, 0], x1.at[k, s]).wait()

        xx[k, 0, pos2[k]] = jnp.dot(take[k], phx[k].reshape(128, PIECE), preferred_element_type=F32).astype(BF16)
        for h in (0, 1):
            onward(k, pos2[k], 0, h)

    @pl.loop(0, R + 1)
    def _(s):
        @pl.when(s + 2 < R)
        def _():
            arrive(s + 2)

        @pl.when(s + 1 < R)
        def _():
            weights(s + 1)

        @pl.when(jnp.logical_and(s > 0, s < R))
        def _():
            relay(s)

        @pl.when(s > 0)
        def _():
            multiply(s - 1)

    hpos, hdev = (z, y), (on_z, on_y)
    ppos, pdev = (y, z), (on_y, on_z)

    def piece(k, p, h):
        return hg.at[k, pl.ds(h * HS, HS), pl.ds(pl.multiple_of(mod(p, R) * 128, 128), 128)]

    done = hacc[...].astype(BF16)
    for k in (0, 1):
        hg[k, :, pl.ds(pl.multiple_of(hpos[k] * 128, 128), 128)] = done
    for h in (0, 1):
        for k in (0, 1):
            blk = piece(k, hpos[k], h)
            remote(blk, blk, hs.at[k, h, 0], hr.at[k, h, 1], hdev[k](hpos[k] + d)).start()
            remote(blk, blk, hs.at[k, h, 1], hr.at[k, h, 2], hdev[k](hpos[k] - d)).start()

    def pass_on(h, s):
        way, far = travel(s)
        for k in (0, 1):
            blk = piece(k, hpos[k] - way * far, h)
            waiter(blk, hr.at[k, h, s]).wait()

            @pl.when(s <= 5)
            def _():
                remote(blk, blk, hs.at[k, h, s + 1], hr.at[k, h, s + 2], hdev[k](hpos[k] + way)).start()

    def partial(h):
        for k in (0, 1):
            for n in range(3):
                part = across(wab[k].reshape(R * HALF, 1024), hg[k, pl.ds(h * HS + n * 128, 128), :])
                psend[k, h, :, :, pl.ds(n * 128, 128)] = part.astype(BF16).reshape(R, HALF, 128)

            @pl.loop(1, R)
            def _(j):
                to = mod(ppos[k] + j, R)
                remote(psend.at[k, h, to], precv.at[k, h, ppos[k]], ps.at[k, h], pr.at[k, h], pdev[k](to)).start()

    mine = e == y
    landing = frecv.at[z * R + e]

    def finish(h):
        for k in (0, 1):
            waiter(precv.at[k, h, pl.ds(0, R - 1)], pr.at[k, h]).wait()
            precv[k, h, ppos[k]] = psend[k, h, ppos[k]]
            total = precv[k, h, 0].astype(F32)
            for j in range(1, R):
                total += precv[k, h, j].astype(F32)
            sumt[h, pl.ds(k * HALF, HALF), :] = total.astype(BF16)
        fsend[pl.ds(h * 32, 32)] = across(order[...], sumt[h]).astype(BF16).reshape(32, 16, 128)

        @pl.loop(h * 32, h * 32 + 32)
        def _(b):
            stays = jnp.logical_and(b == t, mine)

            @pl.when(stays)
            def _():
                pltpu.make_async_copy(fsend.at[b], landing, fr).start()

            @pl.when(jnp.logical_not(stays))
            def _():
                remote(fsend.at[b], landing, fs, fr, (y, b)).start()

    sumt[...] = jnp.zeros_like(sumt)

    @pl.loop(1, R + 2)
    def _(s):
        @pl.when(s < R)
        def _():
            pass_on(0, s)

        @pl.when(s == R - 1)
        def _():
            pass_on(1, s - 2)
            for k in (0, 1):
                waiter(wab.at[k], wr.at[k]).wait()
            partial(0)

        @pl.when(jnp.logical_and(s > 2, s != R - 1))
        def _():
            pass_on(1, s - 2)

    partial(1)
    finish(0)
    finish(1)

    waiter(frecv, fr).wait()
    for n in range(R):
        got = frecv[pl.ds(n * R, R)].reshape(128, 128).astype(F32)
        mixed = jnp.dot(wall[...], got, precision=lax.Precision.HIGHEST, preferred_element_type=F32)
        out_ref[:, pl.ds(n * 128, 128)] = mixed.astype(BF16)

    @pl.loop(0, R - 1)
    def _(s):
        for k in (0, 1):
            waiter(ph1.at[k, 0], s1.at[k, s]).wait()
            for h in (0, 1):
                waiter(xin.at[k, 0, pl.ds(0, CUT)], s2.at[k, h, s]).wait()
                waiter(piece(k, 0, h), hs.at[k, h, s]).wait()

    @pl.loop(0, R)
    def _(s):
        for k in (0, 1):
            waiter(phx.at[k, 0], y1.at[k, s]).wait()
            for h in (0, 1):
                waiter(xs.at[k, 0, pl.ds(0, CUT)], ss.at[k, h, s]).wait()
                waiter(xx.at[k, 0, 0, pl.ds(0, CUT)], sq.at[k, h, s]).wait()

                @pl.when(s > 0)
                def _():
                    waiter(xx.at[k, 0, 0, pl.ds(0, CUT)], sx.at[k, h, s]).wait()

    for k in (0, 1):
        waiter(wab.at[k, pl.ds(0, R - 1)], ws.at[k]).wait()
        for h in (0, 1):
            waiter(psend.at[k, h, pl.ds(0, R - 1)], ps.at[k, h]).wait()

    @pl.when(mine)
    def _():
        waiter(fsend.at[pl.ds(0, R * R - 1)], fs).wait()

    @pl.when(jnp.logical_not(mine))
    def _():
        waiter(fsend, fs).wait()


def local(tokens, expert_ids, gate_units, gate_weight, up_weight, down_weight):
    rows = tokens.shape[0]
    dma = pltpu.SemaphoreType.DMA
    anywhere = pl.BlockSpec(memory_space=pl.ANY)
    vmem = pl.BlockSpec(memory_space=pltpu.VMEM)
    out = pl.pallas_call(
        kernel,
        out_shape=jax.ShapeDtypeStruct((rows, 1024), BF16),
        in_specs=[anywhere, vmem, vmem, anywhere, anywhere, anywhere],
        out_specs=vmem,
        scratch_shapes=[
            pltpu.VMEM((2, R, 16, WIDE), BF16),
            pltpu.VMEM((2, R, 16, PIECE), BF16),
            pltpu.VMEM((2, R, ROWS, WIDE), BF16),
            pltpu.VMEM((2, R, ROWS, OWN), BF16),
            pltpu.VMEM((2, 2, R, ROWS, PIECE), BF16),
            pltpu.VMEM((D, 256), BF16),
            pltpu.VMEM((2, R, HALF, 1024), BF16),
            pltpu.VMEM((SLOTS, 128), F32),
            pltpu.VMEM((2, SLOTS, 1024), BF16),
            pltpu.VMEM((2, 2, R, HALF, HS), BF16),
            pltpu.VMEM((2, 2, R, HALF, HS), BF16),
            pltpu.VMEM((2, 128, HS), BF16),
            pltpu.VMEM((512, HS), BF16),
            pltpu.VMEM((rows, 128), F32),
            pltpu.VMEM((R * R, 16, 128), BF16),
            pltpu.VMEM((R * R, 16, 128), BF16),
            dma((6,)),
            dma((2, R)), dma((2, R)),
            dma((2, R)), dma((2, R)),
            dma((2, 2, R)), dma((2, 2, R)),
            dma((2, 2, R)), dma((2, 2, R)),
            dma((2, 2, R)), dma((2, 2, R)),
            dma((2, 2, R)), dma((2, 2, R)),
            dma((2,)), dma((2,)),
            dma((2, 2, R)), dma((2, 2, R)),
            dma((2, 2)), dma((2, 2)),
            dma, dma,
        ],
        compiler_params=pltpu.CompilerParams(
            collective_id=0, has_side_effects=True, vmem_limit_bytes=60 * 1024 * 1024),
    )(tokens, expert_ids.T, gate_units.T, gate_weight[0], up_weight[0], down_weight[0])
    return out.reshape(rows, R, 128)[:, :, :HALF * 2].reshape(rows, R * HALF * 2)


def solution(mesh):
    return jax.shard_map(
        local,
        mesh=mesh,
        in_specs=(
            P("tensor", None),
            P("tensor", None),
            P("tensor", None),
            P("expert", None, "tensor"),
            P("expert", None, "tensor"),
            P("expert", "tensor", None),
        ),
        out_specs=P("tensor", "expert"),
        check_vma=False,
    )
```

```python
import jax
import jax.numpy as jnp
from jax import lax
from jax.experimental import pallas as pl
from jax.experimental.pallas import tpu as pltpu
from jax.sharding import PartitionSpec as P

MESH = pl.DeviceIdType.MESH
R = 8
NX = 4
D = 6144
PIECE = 1408
BOTH = 256
OWN = PIECE + BOTH
WIDE = OWN + 128
ROWS = 96
CUT = ROWS // 2
SLOTS = 768
HS = SLOTS // 2
HALF = 48
F32, BF16 = jnp.float32, jnp.bfloat16


def mod(a, n):
    return lax.rem(a + 4 * n, n)


def iota(shape, axis):
    return lax.broadcasted_iota(jnp.int32, shape, axis)


def ones(test):
    return jnp.where(test, 1.0, 0.0)


def across(a, b, **how):
    return lax.dot_general(a, b, (((1,), (1,)), ((), ())), preferred_element_type=F32, **how)


def kernel(tok_ref, ids_ref, unit_ref, wg_ref, wu_ref, wd_ref, out_ref,
           ph1, phx, xin, xs, xx, acc, wgu, wab, hacc, hg, psend, precv, sumt, order, wall, fsend, frecv,
           loc, r1, s1, x1, y1, r2, s2, rx, sx, rs, ss, rq, sq, wr, ws, hr, hs, pr, ps, fr, fs):
    e, t = lax.axis_index("expert"), lax.axis_index("tensor")
    y, z = t // R, lax.rem(t, R)
    x, c = e // 2, lax.rem(e, 2)
    d = 1 - 2 * c
    pos1, pos2 = (z, y), (y, z)
    sib = x * 2 + 1 - c
    xdev = (mod(x + 1, NX) * 2 + c, mod(x - 1, NX) * 2 + c)
    quarter = lax.rem(x, 2) * 2 + c

    def on_z(p):
        return (e, y * R + mod(p, R))

    def on_y(p):
        return (e, mod(p, R) * R + z)

    dev1, dev2 = (on_z, on_y), (on_y, on_z)

    def remote(src, dst, send, recv, dev):
        return pltpu.make_async_remote_copy(
            src_ref=src, dst_ref=dst, send_sem=send, recv_sem=recv,
            device_id=dev, device_id_type=MESH)

    def waiter(ref, sem):
        return pltpu.make_async_copy(ref, ref, sem)

    barrier = pltpu.get_barrier_semaphore()
    near = [on(p + hop) for on, p in ((on_z, z), (on_y, y)) for hop in (1, -1, 2, -2)]
    for dev in near + [(xdev[0], t), (xdev[1], t), (sib, t)]:
        pl.semaphore_signal(barrier, inc=1, device_id=dev, device_id_type=MESH)

    first = pl.multiple_of(quarter * PIECE, 128)
    second = pl.multiple_of(4 * PIECE + c * BOTH, 128)
    blocks = []
    for k in (0, 1):
        rows = pl.ds(8 * k, 16)
        blocks.append(pltpu.make_async_copy(
            tok_ref.at[rows, pl.ds(first, PIECE)], ph1.at[k, pos1[k], :, pl.ds(0, PIECE)], loc.at[2 + k]))
        blocks.append(pltpu.make_async_copy(
            tok_ref.at[rows, pl.ds(second, BOTH)], ph1.at[k, pos1[k], :, pl.ds(PIECE, BOTH)], loc.at[4 + k]))
    loads = [pltpu.make_async_copy(wg_ref, wgu.at[:, pl.ds(0, 128)], loc.at[0]),
             pltpu.make_async_copy(wu_ref, wgu.at[:, pl.ds(128, 128)], loc.at[1])]
    for one in blocks + loads:
        one.start()

    tokens = ids_ref.shape[1]
    ids, units = ids_ref[...], unit_ref[...].astype(F32)
    shares = units / (units[0:1, :] + units[1:2, :])
    home = iota((128, tokens), 0) // 16
    named = (ones(home == ids[0:1, :]), ones(home == ids[1:2, :]))
    names = (named[0] + named[1]).astype(BF16)
    here, there = iota((tokens, tokens), 0), iota((tokens, tokens), 1)
    rank = across(ones(there < here).astype(BF16), names)
    used = across(ones(there == here).astype(BF16), names)
    weight = across(ones(there == here), named[0] * shares[0:1, :] + named[1] * shares[1:2, :],
                    precision=lax.Precision.HIGHEST)
    lane = iota((tokens, 128), 1)
    wall[...] = jnp.where(rank == lax.rem(lane, 16).astype(F32), weight, 0.0)
    slot = jnp.sum(jnp.where(lane == e * 16, jnp.where(used > 0.5, rank, -1.0), 0.0), axis=1, keepdims=True)
    tag = jnp.broadcast_to(slot, (tokens, 128))
    for k in (0, 1):
        ph1[k, pos1[k], :, pl.ds(OWN, 128)] = tag[8 * k:8 * k + 16].astype(BF16)

    for one in blocks:
        one.wait()
    pl.semaphore_wait(barrier, 11)

    def travel(s):
        way = jnp.where(s == R - 1, d, 2 * lax.rem(s, 2) - 1)
        return way, (s + 1) // 2

    def goes_on(s):
        return (s <= 4) | ((s == 5) & (c == 0)) | ((s == 6) & (c == 1))

    def later(s):
        return jnp.minimum(s + 2, R - 1)

    def early(k, p, s):
        remote(ph1.at[k, p, :, pl.ds(0, PIECE)], phx.at[k, p], y1.at[k, s], x1.at[k, s], (xdev[k], t)).start()

    def pass_block(k, p, s, to):
        blk = ph1.at[k, p]
        remote(blk, blk, s1.at[k, s - 1], r1.at[k, s], dev1[k](to)).start()

    for k in (0, 1):
        me = pos1[k]
        for s, hop in ((1, 1), (2, -1), (3, 2), (4, -2)):
            pass_block(k, me, s, me + hop)
        early(k, me, 0)

    r = iota((512, HS), 0)
    at = lax.rem(r, 16)
    order[...] = ones(iota((512, HS), 1) == jnp.where(at < 12, (r // 16) * 12 + at, -1)).astype(BF16)

    @pl.loop(1, R)
    def _(s):
        way, far = travel(s)
        for k in (0, 1):
            me = pos1[k]
            p = mod(me - way * far, R)
            waiter(ph1.at[k, p], r1.at[k, s]).wait()

            @pl.when((s == 3) | (s == 4))
            def _():
                pass_block(k, p, s + 2, me + way)

            @pl.when(s == 3 + c)
            def _():
                pass_block(k, p, R - 1, me + 2 * way)

            early(k, p, s)

    row, col = iota((ROWS, 128), 0), iota((ROWS, 128), 1)
    take = [ones(col == (row // 12) * 16 + 4 * k + lax.rem(row, 12)).astype(BF16) for k in (0, 1)]

    def part_of(k, h):
        return pl.ds(k * ROWS + h * CUT, CUT)

    def share(k, s, h):
        rows = part_of(k, h)
        if not isinstance(s, int):
            remote(xin.at[s, rows, pl.ds(0, PIECE)], xx.at[0, s, rows], sx.at[k, h, s], rx.at[k, h, s],
                   (xdev[k], t)).start()
        remote(xin.at[s, rows, pl.ds(0, OWN)], xs.at[s, rows], ss.at[k, h, s], rs.at[k, h, s], (sib, t)).start()

    for k in (0, 1):
        me = pos2[k]
        xin[0, pl.ds(k * ROWS, ROWS)] = jnp.dot(
            take[k], ph1[k].reshape(128, WIDE), preferred_element_type=F32).astype(BF16)
        for h in (0, 1):
            rows = part_of(k, h)
            for s, hop in ((1, 1), (2, -1)):
                remote(xin.at[0, rows], xin.at[s, rows], s2.at[k, h, s - 1], r2.at[k, h, s], dev2[k](me + hop)).start()
    for k in (0, 1):
        for h in (0, 1):
            share(k, 0, h)

    for one in loads:
        one.wait()

    def arrive(s):
        way, far = travel(s)
        for h in (0, 1):
            for k in (0, 1):
                rows = part_of(k, h)
                waiter(xin.at[s, rows], r2.at[k, h, s]).wait()

                @pl.when(goes_on(s))
                def _():
                    remote(xin.at[s, rows], xin.at[later(s), rows], s2.at[k, h, later(s) - 1], r2.at[k, h, later(s)],
                           dev2[k](pos2[k] + way)).start()

                share(k, s, h)

    def weights(k):
        ty, tz = mod(y + k, R), mod(z + k, R)
        remote(wd_ref.at[pl.ds(0, HALF), pl.ds(pl.multiple_of(ty * 1024, 1024), 1024)],
               wab.at[0, y], ws.at[0], wr.at[0], on_y(ty)).start()
        for j in range(R):
            remote(wd_ref.at[pl.ds(HALF, HALF), pl.ds(pl.multiple_of(j * 1024 + tz * 128, 128), 128)],
                   wab.at[1, z, :, pl.ds(j * 128, 128)], ws.at[1], wr.at[1], on_z(tz)).start()

    pltpu.make_async_copy(wd_ref.at[pl.ds(0, HALF), pl.ds(pl.multiple_of(y * 1024, 1024), 1024)],
                          wab.at[0, y], wr.at[0]).start()
    for j in range(R):
        pltpu.make_async_copy(wd_ref.at[pl.ds(HALF, HALF), pl.ds(pl.multiple_of(j * 1024 + z * 128, 128), 128)],
                              wab.at[1, z, :, pl.ds(j * 128, 128)], wr.at[1]).start()

    hacc[...] = jnp.zeros_like(hacc)

    def onward(k, s, h):
        rows = part_of(k, h)
        remote(xx.at[0, s, rows], xx.at[1, s, rows], sq.at[k, h, s], rq.at[k, h, s], (sib, t)).start()

    def relay(s):
        for h in (0, 1):
            for k in (0, 1):
                waiter(xx.at[0, s, part_of(k, h)], rx.at[k, h, s]).wait()
                onward(k, s, h)

    def part(rows, q, size=PIECE):
        return jnp.dot(rows, wgu[pl.ds(pl.multiple_of(q, 128), size), :], preferred_element_type=F32)

    beside, over = quarter + 1 - 2 * c, lax.rem(quarter + 2, 4)

    def multiply_plane(s):
        for k in (0, 1):
            for h in (0, 1):
                waiter(xs.at[s, part_of(k, h)], rs.at[k, h, s]).wait()
        some = part(xin[s, :, pl.ds(0, PIECE)], quarter * PIECE)
        some += part(xin[s, :, pl.ds(PIECE, BOTH)], second, BOTH)
        some += part(xs[s, :, pl.ds(0, PIECE)], beside * PIECE)
        some += part(xs[s, :, pl.ds(PIECE, BOTH)], 4 * PIECE + (1 - c) * BOTH, BOTH)
        acc[s] = some

    def multiply(s):
        way, far = travel(s)
        for k in (0, 1):
            for h in (0, 1):
                waiter(xx.at[1, s, part_of(k, h)], rq.at[k, h, s]).wait()
        both = acc[s] + part(xx[0, s], over * PIECE)
        both += part(xx[1, s], (over + 1 - 2 * c) * PIECE)
        gate, up = both[:, :128], both[:, 128:]
        hidden = (gate / (1.0 + jnp.exp(-gate)) * up).astype(BF16)
        place = xin[s, :, pl.ds(OWN, 128)].astype(F32)[:, 0:1]
        at = iota((2 * ROWS, 1), 0)
        line = lax.rem(at, ROWS) // 12
        block = jnp.where(at < ROWS, mod(y - way * far, R) * R + line, line * R + mod(z - way * far, R))
        goal = jnp.where(place >= 0, block.astype(F32) * 12.0 + place, -1.0)
        chosen = ones(iota((2 * ROWS, SLOTS), 1).astype(F32) == goal).astype(BF16)
        hacc[...] += lax.dot_general(chosen, hidden, (((0,), (0,)), ((), ())), preferred_element_type=F32)

    arrive(jnp.int32(1))

    for k in (0, 1):
        @pl.loop(0, R)
        def _(s):
            waiter(phx.at[k, 0], x1.at[k, s]).wait()

        xx[0, 0, pl.ds(k * ROWS, ROWS)] = jnp.dot(
            take[k], phx[k].reshape(128, PIECE), preferred_element_type=F32).astype(BF16)
        for h in (0, 1):
            onward(k, 0, h)

    @pl.loop(0, R + 1)
    def _(s):
        @pl.when(s + 2 < R)
        def _():
            arrive(s + 2)

        @pl.when(s + 1 < R)
        def _():
            weights(s + 1)

        @pl.when(s < R)
        def _():
            multiply_plane(s)

        @pl.when(s > 0)
        def _():
            multiply(s - 1)

        @pl.when(jnp.logical_and(s > 0, s < R))
        def _():
            relay(s)

    hpos, hdev = (z, y), (on_z, on_y)
    ppos, pdev = (y, z), (on_y, on_z)

    def piece(k, p, h):
        return hg.at[k, pl.ds(h * HS, HS), pl.ds(pl.multiple_of(mod(p, R) * 128, 128), 128)]

    done = hacc[...].astype(BF16)
    for k in (0, 1):
        hg[k, :, pl.ds(pl.multiple_of(hpos[k] * 128, 128), 128)] = done
    for h in (0, 1):
        for k in (0, 1):
            blk = piece(k, hpos[k], h)
            for s, hop in ((1, 1), (2, -1)):
                remote(blk, blk, hs.at[k, h, s - 1], hr.at[k, h, s], hdev[k](hpos[k] + hop)).start()

    def pass_on(h, s):
        way, far = travel(s)
        for k in (0, 1):
            blk = piece(k, hpos[k] - way * far, h)
            waiter(blk, hr.at[k, h, s]).wait()

            @pl.when(goes_on(s))
            def _():
                remote(blk, blk, hs.at[k, h, later(s) - 1], hr.at[k, h, later(s)], hdev[k](hpos[k] + way)).start()

    def send_sum(k, h, q, far):
        way = 1 - 2 * q
        remote(psend.at[k, h, mod(ppos[k] + way * far, R)], precv.at[k, h, q, far - 1],
               ps.at[k, h, q * 4 + far - 1], pr.at[k, h, q * 4 + far - 1], pdev[k](ppos[k] + way)).start()

    def partial(h):
        for k in (0, 1):
            some = across(wab[k].reshape(R * HALF, 1024), hg[k, pl.ds(h * HS, HS), :])
            psend[k, h] = some.astype(BF16).reshape(R, HALF, HS)
            for q in (0, 1):
                @pl.when(c == q)
                def _():
                    send_sum(k, h, q, 4)

                @pl.when(c != q)
                def _():
                    send_sum(k, h, q, 3)

    def add_on(h, far):
        for k in (0, 1):
            for q in (0, 1):
                @pl.when((far < 3) | (c == q))
                def _():
                    own = mod(ppos[k] + (1 - 2 * q) * far, R)
                    waiter(precv.at[k, h, q, far], pr.at[k, h, q * 4 + far]).wait()
                    psend[k, h, own] = (psend[k, h, own].astype(F32) + precv[k, h, q, far].astype(F32)).astype(BF16)
                    send_sum(k, h, q, far)

    mine = e == y
    landing = frecv.at[z * R + e]

    def finish(h):
        for k in (0, 1):
            total = psend[k, h, ppos[k]].astype(F32)
            for q in (0, 1):
                waiter(precv.at[k, h, q, 0], pr.at[k, h, q * 4]).wait()
                total += precv[k, h, q, 0].astype(F32)
            sumt[h, pl.ds(k * HALF, HALF), :] = total.astype(BF16)
        fsend[pl.ds(h * 32, 32)] = across(order[...], sumt[h]).astype(BF16).reshape(32, 16, 128)

        @pl.loop(0, 32)
        def _(i):
            b = h * 32 + lax.rem(y + 2 + i // R, 4) * R + lax.rem(z + 4 + i, R)
            stays = jnp.logical_and(b == t, mine)

            @pl.when(stays)
            def _():
                pltpu.make_async_copy(fsend.at[b], landing, fr).start()

            @pl.when(jnp.logical_not(stays))
            def _():
                remote(fsend.at[b], landing, fs, fr, (y, b)).start()

    sumt[...] = jnp.zeros_like(sumt)

    @pl.loop(0, 3)
    def _(i):
        for h in (0, 1):
            pass_on(h, 2 * i + 1)
            pass_on(h, 2 * i + 2)

    pass_on(0, jnp.int32(R - 1))
    for k in (0, 1):
        waiter(wab.at[k], wr.at[k]).wait()
    partial(0)
    pass_on(1, jnp.int32(R - 1))
    partial(1)
    for far in (3, 2, 1):
        for h in (0, 1):
            add_on(h, far)
    finish(0)
    finish(1)

    left, terms = wall[...], []
    for _ in range(3):
        terms.append(left.astype(BF16).astype(F32))
        left = left - terms[-1]
    terms = jnp.concatenate(terms, axis=0).astype(BF16)
    waiter(frecv, fr).wait()
    for n in range(R):
        mixed = jnp.dot(terms, frecv[pl.ds(n * R, R)].reshape(128, 128), preferred_element_type=F32)
        mixed = mixed[:tokens] + mixed[tokens:2 * tokens] + mixed[2 * tokens:]
        out_ref[:, pl.ds(n * 128, 128)] = mixed.astype(BF16)

    @pl.loop(0, R - 1)
    def _(s):
        for k in (0, 1):
            waiter(ph1.at[k, 0], s1.at[k, s]).wait()
            for h in (0, 1):
                waiter(xin.at[0, pl.ds(0, CUT)], s2.at[k, h, s]).wait()
                waiter(piece(k, 0, h), hs.at[k, h, s]).wait()

    @pl.loop(0, R)
    def _(s):
        for k in (0, 1):
            waiter(phx.at[k, 0], y1.at[k, s]).wait()
            for h in (0, 1):
                waiter(xs.at[0, pl.ds(0, CUT)], ss.at[k, h, s]).wait()
                waiter(xx.at[0, 0, pl.ds(0, CUT)], sq.at[k, h, s]).wait()

                @pl.when(s > 0)
                def _():
                    waiter(xx.at[0, 0, pl.ds(0, CUT)], sx.at[k, h, s]).wait()

    for k in (0, 1):
        waiter(wab.at[k, pl.ds(0, R - 1)], ws.at[k]).wait()
        for h in (0, 1):
            for q in (0, 1):
                for far in (0, 1, 2):
                    waiter(psend.at[k, h, 0], ps.at[k, h, q * 4 + far]).wait()

                @pl.when(c == q)
                def _():
                    waiter(psend.at[k, h, 0], ps.at[k, h, q * 4 + 3]).wait()

    @pl.when(mine)
    def _():
        waiter(fsend.at[pl.ds(0, R * R - 1)], fs).wait()

    @pl.when(jnp.logical_not(mine))
    def _():
        waiter(fsend, fs).wait()


def local(tokens, expert_ids, gate_units, gate_weight, up_weight, down_weight):
    rows = tokens.shape[0]
    dma = pltpu.SemaphoreType.DMA
    anywhere = pl.BlockSpec(memory_space=pl.ANY)
    vmem = pl.BlockSpec(memory_space=pltpu.VMEM)
    out = pl.pallas_call(
        kernel,
        out_shape=jax.ShapeDtypeStruct((rows, 1024), BF16),
        in_specs=[anywhere, vmem, vmem, anywhere, anywhere, anywhere],
        out_specs=vmem,
        scratch_shapes=[
            pltpu.VMEM((2, R, 16, WIDE), BF16),
            pltpu.VMEM((2, R, 16, PIECE), BF16),
            pltpu.VMEM((R, 2 * ROWS, WIDE), BF16),
            pltpu.VMEM((R, 2 * ROWS, OWN), BF16),
            pltpu.VMEM((2, R, 2 * ROWS, PIECE), BF16),
            pltpu.VMEM((R, 2 * ROWS, 256), F32),
            pltpu.VMEM((D, 256), BF16),
            pltpu.VMEM((2, R, HALF, 1024), BF16),
            pltpu.VMEM((SLOTS, 128), F32),
            pltpu.VMEM((2, SLOTS, 1024), BF16),
            pltpu.VMEM((2, 2, R, HALF, HS), BF16),
            pltpu.VMEM((2, 2, 2, 4, HALF, HS), BF16),
            pltpu.VMEM((2, 128, HS), BF16),
            pltpu.VMEM((512, HS), BF16),
            pltpu.VMEM((rows, 128), F32),
            pltpu.VMEM((R * R, 16, 128), BF16),
            pltpu.VMEM((R * R, 16, 128), BF16),
            dma((6,)),
            dma((2, R)), dma((2, R)),
            dma((2, R)), dma((2, R)),
            dma((2, 2, R)), dma((2, 2, R)),
            dma((2, 2, R)), dma((2, 2, R)),
            dma((2, 2, R)), dma((2, 2, R)),
            dma((2, 2, R)), dma((2, 2, R)),
            dma((2,)), dma((2,)),
            dma((2, 2, R)), dma((2, 2, R)),
            dma((2, 2, 8)), dma((2, 2, 8)),
            dma, dma,
        ],
        compiler_params=pltpu.CompilerParams(
            collective_id=0, has_side_effects=True, vmem_limit_bytes=60 * 1024 * 1024),
    )(tokens, expert_ids.T, gate_units.T, gate_weight[0], up_weight[0], down_weight[0])
    return out.reshape(rows, R, 128)[:, :, :HALF * 2].reshape(rows, R * HALF * 2)


def solution(mesh):
    return jax.shard_map(
        local,
        mesh=mesh,
        in_specs=(
            P("tensor", None),
            P("tensor", None),
            P("tensor", None),
            P("expert", None, "tensor"),
            P("expert", None, "tensor"),
            P("expert", "tensor", None),
        ),
        out_specs=P("tensor", "expert"),
        check_vma=False,
    )
```

```python
import jax
import jax.numpy as jnp
from jax import lax
from jax.experimental import pallas as pl
from jax.experimental.pallas import tpu as pltpu
from jax.sharding import PartitionSpec as P

MESH = pl.DeviceIdType.MESH
R = 8
NX = 4
D = 6144
PIECE = 1408
BOTH = 256
OWN = PIECE + BOTH
WIDE = OWN + 128
ROWS = 96
CUT = ROWS // 2
SLOTS = 768
HS = SLOTS // 2
HALF = 48
F32, BF16 = jnp.float32, jnp.bfloat16


def mod(a, n):
    return lax.rem(a + 4 * n, n)


def iota(shape, axis):
    return lax.broadcasted_iota(jnp.int32, shape, axis)


def ones(test):
    return jnp.where(test, 1.0, 0.0)


def across(a, b, **how):
    return lax.dot_general(a, b, (((1,), (1,)), ((), ())), preferred_element_type=F32, **how)


def kernel(tok_ref, ids_ref, unit_ref, wg_ref, wu_ref, wd_ref, out_ref,
           ph1, phx, xin, xs, xx, acc, wgu, wab, hacc, hg, psend, precv, sumt, order, wall, fsend, frecv,
           loc, r1, s1, x1, y1, r2, s2, rx, sx, rs, ss, rq, sq, wr, ws, hr, hs, pr, ps, fr, fs):
    e, t = lax.axis_index("expert"), lax.axis_index("tensor")
    y, z = t // R, lax.rem(t, R)
    x, c = e // 2, lax.rem(e, 2)
    d = 1 - 2 * c
    pos1, pos2 = (z, y), (y, z)
    sib = x * 2 + 1 - c
    xdev = (mod(x + 1, NX) * 2 + c, mod(x - 1, NX) * 2 + c)
    quarter = lax.rem(x, 2) * 2 + c

    def on_z(p):
        return (e, y * R + mod(p, R))

    def on_y(p):
        return (e, mod(p, R) * R + z)

    dev1, dev2 = (on_z, on_y), (on_y, on_z)

    def remote(src, dst, send, recv, dev):
        return pltpu.make_async_remote_copy(
            src_ref=src, dst_ref=dst, send_sem=send, recv_sem=recv,
            device_id=dev, device_id_type=MESH)

    def waiter(ref, sem):
        return pltpu.make_async_copy(ref, ref, sem)

    barrier = pltpu.get_barrier_semaphore()
    near = [on(p + hop) for on, p in ((on_z, z), (on_y, y)) for hop in (1, -1, 2, -2)]
    for dev in near + [(xdev[0], t), (xdev[1], t), (sib, t)]:
        pl.semaphore_signal(barrier, inc=1, device_id=dev, device_id_type=MESH)

    first = pl.multiple_of(quarter * PIECE, 128)
    second = pl.multiple_of(4 * PIECE + c * BOTH, 128)
    blocks = []
    for k in (0, 1):
        rows = pl.ds(8 * k, 16)
        blocks.append(pltpu.make_async_copy(
            tok_ref.at[rows, pl.ds(first, PIECE)], ph1.at[k, pos1[k], :, pl.ds(0, PIECE)], loc.at[2 + k]))
        blocks.append(pltpu.make_async_copy(
            tok_ref.at[rows, pl.ds(second, BOTH)], ph1.at[k, pos1[k], :, pl.ds(PIECE, BOTH)], loc.at[4 + k]))
    loads = [pltpu.make_async_copy(wg_ref, wgu.at[:, pl.ds(0, 128)], loc.at[0]),
             pltpu.make_async_copy(wu_ref, wgu.at[:, pl.ds(128, 128)], loc.at[1])]
    for one in blocks + loads:
        one.start()

    tokens = ids_ref.shape[1]
    ids, units = ids_ref[...], unit_ref[...].astype(F32)
    shares = units / (units[0:1, :] + units[1:2, :])
    home = iota((128, tokens), 0) // 16
    named = (ones(home == ids[0:1, :]), ones(home == ids[1:2, :]))
    names = (named[0] + named[1]).astype(BF16)
    here, there = iota((tokens, tokens), 0), iota((tokens, tokens), 1)
    rank = across(ones(there < here).astype(BF16), names)
    used = across(ones(there == here).astype(BF16), names)
    weight = across(ones(there == here), named[0] * shares[0:1, :] + named[1] * shares[1:2, :],
                    precision=lax.Precision.HIGHEST)
    lane = iota((tokens, 128), 1)
    wall[...] = jnp.where(rank == lax.rem(lane, 16).astype(F32), weight, 0.0)
    slot = jnp.sum(jnp.where(lane == e * 16, jnp.where(used > 0.5, rank, -1.0), 0.0), axis=1, keepdims=True)
    tag = jnp.broadcast_to(slot, (tokens, 128))
    for k in (0, 1):
        ph1[k, pos1[k], :, pl.ds(OWN, 128)] = tag[8 * k:8 * k + 16].astype(BF16)

    for one in blocks:
        one.wait()
    pl.semaphore_wait(barrier, 11)

    def travel(s):
        way = jnp.where(s == R - 1, d, 2 * lax.rem(s, 2) - 1)
        return way, (s + 1) // 2

    def goes_on(s):
        return (s <= 4) | ((s == 5) & (c == 0)) | ((s == 6) & (c == 1))

    def later(s):
        return jnp.minimum(s + 2, R - 1)

    def early(k, p, s):
        remote(ph1.at[k, p, :, pl.ds(0, PIECE)], phx.at[k, p], y1.at[k, s], x1.at[k, s], (xdev[k], t)).start()

    def pass_block(k, p, s, to):
        blk = ph1.at[k, p]
        remote(blk, blk, s1.at[k, s - 1], r1.at[k, s], dev1[k](to)).start()

    for k in (0, 1):
        me = pos1[k]
        for s, hop in ((1, 1), (2, -1), (3, 2), (4, -2)):
            pass_block(k, me, s, me + hop)
        early(k, me, 0)

    r = iota((512, HS), 0)
    at = lax.rem(r, 16)
    order[...] = ones(iota((512, HS), 1) == jnp.where(at < 12, (r // 16) * 12 + at, -1)).astype(BF16)

    @pl.loop(1, R)
    def _(s):
        way, far = travel(s)
        for k in (0, 1):
            me = pos1[k]
            p = mod(me - way * far, R)
            waiter(ph1.at[k, p], r1.at[k, s]).wait()

            @pl.when((s == 3) | (s == 4))
            def _():
                pass_block(k, p, s + 2, me + way)

            @pl.when(s == 3 + c)
            def _():
                pass_block(k, p, R - 1, me + 2 * way)

            early(k, p, s)

    row, col = iota((ROWS, 128), 0), iota((ROWS, 128), 1)
    take = [ones(col == (row // 12) * 16 + 4 * k + lax.rem(row, 12)).astype(BF16) for k in (0, 1)]

    def part_of(k, h):
        return pl.ds(k * ROWS + h * CUT, CUT)

    def share(k, s, h):
        rows = part_of(k, h)
        if not isinstance(s, int):
            remote(xin.at[s, rows, pl.ds(0, PIECE)], xx.at[0, s, rows], sx.at[k, h, s], rx.at[k, h, s],
                   (xdev[k], t)).start()
        remote(xin.at[s, rows, pl.ds(0, OWN)], xs.at[s, rows], ss.at[k, h, s], rs.at[k, h, s], (sib, t)).start()

    for k in (0, 1):
        me = pos2[k]
        xin[0, pl.ds(k * ROWS, ROWS)] = jnp.dot(
            take[k], ph1[k].reshape(128, WIDE), preferred_element_type=F32).astype(BF16)
        for h in (0, 1):
            rows = part_of(k, h)
            for s, hop in ((1, 1), (2, -1)):
                remote(xin.at[0, rows], xin.at[s, rows], s2.at[k, h, s - 1], r2.at[k, h, s], dev2[k](me + hop)).start()
    for k in (0, 1):
        for h in (0, 1):
            share(k, 0, h)

    for one in loads:
        one.wait()

    def arrive(s):
        way, far = travel(s)
        for h in (0, 1):
            for k in (0, 1):
                rows = part_of(k, h)
                waiter(xin.at[s, rows], r2.at[k, h, s]).wait()

                @pl.when(goes_on(s))
                def _():
                    remote(xin.at[s, rows], xin.at[later(s), rows], s2.at[k, h, later(s) - 1], r2.at[k, h, later(s)],
                           dev2[k](pos2[k] + way)).start()

                share(k, s, h)

    def weights(k):
        ty, tz = mod(y + k, R), mod(z + k, R)
        remote(wd_ref.at[pl.ds(0, HALF), pl.ds(pl.multiple_of(ty * 1024, 1024), 1024)],
               wab.at[0, y], ws.at[0], wr.at[0], on_y(ty)).start()
        for j in range(R):
            remote(wd_ref.at[pl.ds(HALF, HALF), pl.ds(pl.multiple_of(j * 1024 + tz * 128, 128), 128)],
                   wab.at[1, z, :, pl.ds(j * 128, 128)], ws.at[1], wr.at[1], on_z(tz)).start()

    pltpu.make_async_copy(wd_ref.at[pl.ds(0, HALF), pl.ds(pl.multiple_of(y * 1024, 1024), 1024)],
                          wab.at[0, y], wr.at[0]).start()
    for j in range(R):
        pltpu.make_async_copy(wd_ref.at[pl.ds(HALF, HALF), pl.ds(pl.multiple_of(j * 1024 + z * 128, 128), 128)],
                              wab.at[1, z, :, pl.ds(j * 128, 128)], wr.at[1]).start()

    hacc[...] = jnp.zeros_like(hacc)

    def onward(k, s, h):
        rows = part_of(k, h)
        remote(xx.at[0, s, rows], xx.at[1, s, rows], sq.at[k, h, s], rq.at[k, h, s], (sib, t)).start()

    def relay(s):
        for h in (0, 1):
            for k in (0, 1):
                waiter(xx.at[0, s, part_of(k, h)], rx.at[k, h, s]).wait()
                onward(k, s, h)

    def part(rows, q, size=PIECE):
        return jnp.dot(rows, wgu[pl.ds(pl.multiple_of(q, 128), size), :], preferred_element_type=F32)

    beside, over = quarter + 1 - 2 * c, lax.rem(quarter + 2, 4)

    def multiply_plane(s):
        for k in (0, 1):
            for h in (0, 1):
                waiter(xs.at[s, part_of(k, h)], rs.at[k, h, s]).wait()
        some = part(xin[s, :, pl.ds(0, PIECE)], quarter * PIECE)
        some += part(xin[s, :, pl.ds(PIECE, BOTH)], second, BOTH)
        some += part(xs[s, :, pl.ds(0, PIECE)], beside * PIECE)
        some += part(xs[s, :, pl.ds(PIECE, BOTH)], 4 * PIECE + (1 - c) * BOTH, BOTH)
        acc[s] = some

    def multiply(s):
        way, far = travel(s)
        for k in (0, 1):
            for h in (0, 1):
                waiter(xx.at[1, s, part_of(k, h)], rq.at[k, h, s]).wait()
        both = acc[s] + part(xx[0, s], over * PIECE)
        both += part(xx[1, s], (over + 1 - 2 * c) * PIECE)
        gate, up = both[:, :128], both[:, 128:]
        hidden = (gate / (1.0 + jnp.exp(-gate)) * up).astype(BF16)
        place = xin[s, :, pl.ds(OWN, 128)].astype(F32)[:, 0:1]
        at = iota((2 * ROWS, 1), 0)
        line = lax.rem(at, ROWS) // 12
        block = jnp.where(at < ROWS, mod(y - way * far, R) * R + line, line * R + mod(z - way * far, R))
        goal = jnp.where(place >= 0, block.astype(F32) * 12.0 + place, -1.0)
        chosen = ones(iota((2 * ROWS, SLOTS), 1).astype(F32) == goal).astype(BF16)
        hacc[...] += lax.dot_general(chosen, hidden, (((0,), (0,)), ((), ())), preferred_element_type=F32)

    arrive(jnp.int32(1))

    for k in (0, 1):
        @pl.loop(0, R)
        def _(s):
            waiter(phx.at[k, 0], x1.at[k, s]).wait()

        xx[0, 0, pl.ds(k * ROWS, ROWS)] = jnp.dot(
            take[k], phx[k].reshape(128, PIECE), preferred_element_type=F32).astype(BF16)
        for h in (0, 1):
            onward(k, 0, h)

    @pl.loop(0, R + 1)
    def _(s):
        @pl.when(s + 2 < R)
        def _():
            arrive(s + 2)

        @pl.when(s + 1 < R)
        def _():
            weights(s + 1)

        @pl.when(s < R)
        def _():
            multiply_plane(s)

        @pl.when(s > 0)
        def _():
            multiply(s - 1)

        @pl.when(jnp.logical_and(s > 0, s < R))
        def _():
            relay(s)

    hpos, hdev = (z, y), (on_z, on_y)
    ppos, pdev = (y, z), (on_y, on_z)

    def piece(k, p, h):
        return hg.at[k, pl.ds(h * HS, HS), pl.ds(pl.multiple_of(mod(p, R) * 128, 128), 128)]

    done = hacc[...].astype(BF16)
    for k in (0, 1):
        hg[k, :, pl.ds(pl.multiple_of(hpos[k] * 128, 128), 128)] = done
    for h in (0, 1):
        for k in (0, 1):
            blk = piece(k, hpos[k], h)
            for s, hop in ((1, 1), (2, -1)):
                remote(blk, blk, hs.at[k, h, s - 1], hr.at[k, h, s], hdev[k](hpos[k] + hop)).start()

    def pass_on(h, s):
        way, far = travel(s)
        for k in (0, 1):
            blk = piece(k, hpos[k] - way * far, h)
            waiter(blk, hr.at[k, h, s]).wait()

            @pl.when(goes_on(s))
            def _():
                remote(blk, blk, hs.at[k, h, later(s) - 1], hr.at[k, h, later(s)], hdev[k](hpos[k] + way)).start()

    def send_sum(k, h, q, far):
        way = 1 - 2 * q
        remote(psend.at[k, h, mod(ppos[k] + way * far, R)], precv.at[k, h, q, far - 1],
               ps.at[k, h, q * 4 + far - 1], pr.at[k, h, q * 4 + far - 1], pdev[k](ppos[k] + way)).start()

    def partial(h):
        for k in (0, 1):
            some = across(wab[k].reshape(R * HALF, 1024), hg[k, pl.ds(h * HS, HS), :])
            psend[k, h] = some.astype(BF16).reshape(R, HALF, HS)
            for q in (0, 1):
                @pl.when(c == q)
                def _():
                    send_sum(k, h, q, 4)

                @pl.when(c != q)
                def _():
                    send_sum(k, h, q, 3)

    def add_on(h, far):
        for k in (0, 1):
            for q in (0, 1):
                @pl.when((far < 3) | (c == q))
                def _():
                    own = mod(ppos[k] + (1 - 2 * q) * far, R)
                    waiter(precv.at[k, h, q, far], pr.at[k, h, q * 4 + far]).wait()
                    psend[k, h, own] = (psend[k, h, own].astype(F32) + precv[k, h, q, far].astype(F32)).astype(BF16)
                    send_sum(k, h, q, far)

    mine = e == y
    landing = frecv.at[z * R + e]

    def finish(h):
        for k in (0, 1):
            total = psend[k, h, ppos[k]].astype(F32)
            for q in (0, 1):
                waiter(precv.at[k, h, q, 0], pr.at[k, h, q * 4]).wait()
                total += precv[k, h, q, 0].astype(F32)
            sumt[h, pl.ds(k * HALF, HALF), :] = total.astype(BF16)
        fsend[pl.ds(h * 32, 32)] = across(order[...], sumt[h]).astype(BF16).reshape(32, 16, 128)

        @pl.loop(0, 32)
        def _(i):
            b = h * 32 + lax.rem(y + 2 + i // R, 4) * R + lax.rem(z + 4 + i, R)
            stays = jnp.logical_and(b == t, mine)

            @pl.when(stays)
            def _():
                pltpu.make_async_copy(fsend.at[b], landing, fr).start()

            @pl.when(jnp.logical_not(stays))
            def _():
                remote(fsend.at[b], landing, fs, fr, (y, b)).start()

    sumt[...] = jnp.zeros_like(sumt)

    @pl.loop(0, 3)
    def _(i):
        for h in (0, 1):
            pass_on(h, 2 * i + 1)
            pass_on(h, 2 * i + 2)

    pass_on(0, jnp.int32(R - 1))
    for k in (0, 1):
        waiter(wab.at[k], wr.at[k]).wait()
    partial(0)
    pass_on(1, jnp.int32(R - 1))
    partial(1)
    for far in (3, 2, 1):
        for h in (0, 1):
            add_on(h, far)
    finish(0)
    finish(1)

    left, terms = wall[...], []
    for _ in range(3):
        terms.append(left.astype(BF16).astype(F32))
        left = left - terms[-1]
    terms = jnp.concatenate(terms, axis=0).astype(BF16)
    @pl.loop(0, R - 1)
    def _(s):
        for k in (0, 1):
            waiter(ph1.at[k, 0], s1.at[k, s]).wait()
            for h in (0, 1):
                waiter(xin.at[0, pl.ds(0, CUT)], s2.at[k, h, s]).wait()
                waiter(piece(k, 0, h), hs.at[k, h, s]).wait()

    @pl.loop(0, R)
    def _(s):
        for k in (0, 1):
            waiter(phx.at[k, 0], y1.at[k, s]).wait()
            for h in (0, 1):
                waiter(xs.at[0, pl.ds(0, CUT)], ss.at[k, h, s]).wait()
                waiter(xx.at[0, 0, pl.ds(0, CUT)], sq.at[k, h, s]).wait()

                @pl.when(s > 0)
                def _():
                    waiter(xx.at[0, 0, pl.ds(0, CUT)], sx.at[k, h, s]).wait()

    for k in (0, 1):
        waiter(wab.at[k, pl.ds(0, R - 1)], ws.at[k]).wait()
        for h in (0, 1):
            for q in (0, 1):
                for far in (0, 1, 2):
                    waiter(psend.at[k, h, 0], ps.at[k, h, q * 4 + far]).wait()

                @pl.when(c == q)
                def _():
                    waiter(psend.at[k, h, 0], ps.at[k, h, q * 4 + 3]).wait()

    waiter(frecv, fr).wait()
    parts = []
    for n in range(R):
        mixed = jnp.dot(terms, frecv[pl.ds(n * R, R)].reshape(128, 128), preferred_element_type=F32)
        mixed = mixed[:tokens] + mixed[tokens:2 * tokens] + mixed[2 * tokens:]
        parts.append(mixed[:, :2 * HALF])
    out_ref[...] = jnp.concatenate(parts, axis=1).astype(BF16)

    @pl.when(mine)
    def _():
        waiter(fsend.at[pl.ds(0, R * R - 1)], fs).wait()

    @pl.when(jnp.logical_not(mine))
    def _():
        waiter(fsend, fs).wait()


def local(tokens, expert_ids, gate_units, gate_weight, up_weight, down_weight):
    rows = tokens.shape[0]
    dma = pltpu.SemaphoreType.DMA
    anywhere = pl.BlockSpec(memory_space=pl.ANY)
    vmem = pl.BlockSpec(memory_space=pltpu.VMEM)
    out = pl.pallas_call(
        kernel,
        out_shape=jax.ShapeDtypeStruct((rows, R * HALF * 2), BF16),
        in_specs=[anywhere, vmem, vmem, anywhere, anywhere, anywhere],
        out_specs=vmem,
        scratch_shapes=[
            pltpu.VMEM((2, R, 16, WIDE), BF16),
            pltpu.VMEM((2, R, 16, PIECE), BF16),
            pltpu.VMEM((R, 2 * ROWS, WIDE), BF16),
            pltpu.VMEM((R, 2 * ROWS, OWN), BF16),
            pltpu.VMEM((2, R, 2 * ROWS, PIECE), BF16),
            pltpu.VMEM((R, 2 * ROWS, 256), F32),
            pltpu.VMEM((D, 256), BF16),
            pltpu.VMEM((2, R, HALF, 1024), BF16),
            pltpu.VMEM((SLOTS, 128), F32),
            pltpu.VMEM((2, SLOTS, 1024), BF16),
            pltpu.VMEM((2, 2, R, HALF, HS), BF16),
            pltpu.VMEM((2, 2, 2, 4, HALF, HS), BF16),
            pltpu.VMEM((2, 128, HS), BF16),
            pltpu.VMEM((512, HS), BF16),
            pltpu.VMEM((rows, 128), F32),
            pltpu.VMEM((R * R, 16, 128), BF16),
            pltpu.VMEM((R * R, 16, 128), BF16),
            dma((6,)),
            dma((2, R)), dma((2, R)),
            dma((2, R)), dma((2, R)),
            dma((2, 2, R)), dma((2, 2, R)),
            dma((2, 2, R)), dma((2, 2, R)),
            dma((2, 2, R)), dma((2, 2, R)),
            dma((2, 2, R)), dma((2, 2, R)),
            dma((2,)), dma((2,)),
            dma((2, 2, R)), dma((2, 2, R)),
            dma((2, 2, 8)), dma((2, 2, 8)),
            dma, dma,
        ],
        compiler_params=pltpu.CompilerParams(
            collective_id=0, has_side_effects=True, vmem_limit_bytes=60 * 1024 * 1024),
    )(tokens, expert_ids.T, gate_units.T, gate_weight[0], up_weight[0], down_weight[0])
    return out


def solution(mesh):
    return jax.shard_map(
        local,
        mesh=mesh,
        in_specs=(
            P("tensor", None),
            P("tensor", None),
            P("tensor", None),
            P("expert", None, "tensor"),
            P("expert", None, "tensor"),
            P("expert", "tensor", None),
        ),
        out_specs=P("tensor", "expert"),
        check_vma=False,
    )
```
